32 devices in a mesh: groups: 2 (over y), row: 8 (over z, x), col: 2 (over core).
Axes of the slice: x: 2, y: 2, z: 4, core: 2. Of those that a mesh axis runs over, the one named last changes fastest.
Arguments:
- tokens: bfloat16 [512, 8192], P(('groups', 'col'), 'row'), parts along dimension 0, may hold values from -6 to 6
- w_up: bfloat16 [8192, 32768], P('col', 'row'), may hold values from -0.125 to 0.125
- w_down: bfloat16 [32768, 8192], P('row', 'col'), may hold values from -0.0625 to 0.0625
- mask_up: int32 [64, 256], P(None, 'row'), may hold values 0 or 1
- mask_down: int32 [256, 64], P('row'), may hold values 0 or 1
Outputs:
- mixed: bfloat16 [512, 8192], P(('groups', 'col', 'row')), parts along dimension 0
The draws below stay inside these ranges and needn't reach their ends.
There are 2 independent parts, one for each index of `groups`. The reference program is written for one: setup_inputs(seed, part) draws one part's arguments, and reference() takes and returns one part's arrays. A program takes and returns all parts, laid end to end along the dimension named above; an argument that names none is the same for every part. Nothing has to cross between parts.
All inputs are finite; a program needn't handle non-finite values. No bound on the sum of `mask_up` or of `mask_down` on one device may be relied on, other than what follows from the above.
Results may differ from the reference program's by a relative error of at most 0.005.
Values may be sent and summed in bfloat16 or wider, within the bound.
A program may use at most 512 MiB of HBM per device.

```python
import jax
import jax.numpy as jnp

D = 8192
FF = 32768
BLK = 128
TOKENS = 256
DB = 64
FB = 256


def with_ends(drawn, rng, smallest, largest):
    place = [jax.random.randint(jax.random.fold_in(rng, axis), (), 0, length) for axis, length in enumerate(drawn.shape)]
    longest = drawn.shape.index(max(drawn.shape))
    next_to = place[:longest] + [(place[longest] + 1) % drawn.shape[longest]] + place[longest + 1:]
    return drawn.at[tuple(place)].set(smallest).at[tuple(next_to)].set(largest)


def steps_of(rng, shape, shards, smallest, top_value):
    level = 1.0
    for dim, shards_of in shards:
        heights = jax.random.uniform(jax.random.fold_in(jax.random.fold_in(rng, 6), dim), (shards_of,), jnp.float32, smallest / len(shards), top_value / len(shards))
        level = level * jnp.repeat(jnp.exp(heights), shape[dim] // shards_of).reshape((-1,) + (1,) * (len(shape) - 1 - dim))
    return level


def gaussian(rng, shape, width, limit, split=(), kind=jnp.bfloat16):
    drawn = jax.random.normal(rng, shape, jnp.float32) * width
    if len(split) > 0:
        drawn = steps_of(rng, shape, split, -0.22, 0.18) * drawn
    return jnp.clip(drawn, min=-limit, max=limit).astype(kind)


def setup_inputs(seed: int = 0, part: int = 0) -> dict:
    seeds = jax.random.split(jax.random.key(seed), 6)
    part_keys = jax.random.split(jax.random.fold_in(seeds[5], part), 6)
    return {
        "tokens": gaussian(part_keys[0], (TOKENS, D), 1.0, 6.0, ((0, 2), (1, 8))),
        "w_up": gaussian(seeds[1], (D, FF), (D // 4) ** -0.5, 0.125, ((0, 2), (1, 8))),
        "w_down": gaussian(seeds[2], (FF, D), (FF // 4) ** -0.5, 0.0625, ((0, 8), (1, 2))),
        "mask_up": with_ends((jax.random.randint(seeds[3], (DB, FB), 0, 4) < 1).astype(jnp.int32), jax.random.fold_in(seeds[3], 1), 0, 1),
        "mask_down": with_ends((jax.random.randint(seeds[4], (FB, DB), 0, 4) < 1).astype(jnp.int32), jax.random.fold_in(seeds[4], 1), 0, 1),
    }


def apply_mask(weight, mask):
    rows, cols = weight.shape
    blocks = weight.reshape(mask.shape[0], BLK, mask.shape[1], BLK)
    kept = blocks * mask.astype(weight.dtype)[:, None, :, None]
    return kept.reshape(rows, cols)


def reference(tokens, w_up, w_down, mask_up, mask_down):
    up_masked = apply_mask(w_up, mask_up)
    pre = jnp.dot(tokens, up_masked, preferred_element_type=jnp.float32)
    hidden = jax.nn.gelu(pre, approximate=False).astype(jnp.bfloat16)
    down_masked = apply_mask(w_down, mask_down)
    return jnp.dot(hidden, down_masked, preferred_element_type=jnp.float32).astype(jnp.bfloat16)
```

```python
import functools

import jax
import jax.numpy as jnp
from jax import lax
from jax.experimental import pallas as pl
from jax.experimental.pallas import tpu as pltpu
from jax.sharding import PartitionSpec as P


def expand_mask(mask, block, dtype):
    count_r, count_c = mask.shape
    wide = jnp.broadcast_to(mask.astype(dtype)[:, None, :, None], (count_r, block, count_c, block))
    return wide.reshape(count_r * block, count_c * block)


def general(tokens, w_up, w_down, mask_up, mask_down):
    cols = lax.axis_size("col")
    block = w_up.shape[0] * cols // mask_up.shape[0]
    core = lax.axis_index("col")
    mine = lax.all_gather(tokens, "row", axis=1, tiled=True)
    x = lax.all_to_all(mine, "col", split_axis=1, concat_axis=0, tiled=True)
    half = mask_up.shape[0] // cols
    mask_u = lax.dynamic_slice_in_dim(mask_up, core * half, half, 0)
    pre = jnp.dot(
        x, w_up * expand_mask(mask_u, block, w_up.dtype), preferred_element_type=jnp.float32
    )
    swap = [(i, (i + 1) % cols) for i in range(cols)]
    pre = pre + lax.ppermute(pre.astype(jnp.bfloat16), "col", swap).astype(jnp.float32)
    hidden = jax.nn.gelu(pre, approximate=False).astype(jnp.bfloat16)
    half_d = mask_down.shape[1] // cols
    mask_d = lax.dynamic_slice_in_dim(mask_down, core * half_d, half_d, 1)
    part = jnp.dot(
        hidden,
        w_down * expand_mask(mask_d, block, w_down.dtype),
        preferred_element_type=jnp.float32,
    )
    part = lax.all_to_all(
        part.astype(jnp.bfloat16), "col", split_axis=0, concat_axis=1, tiled=True
    )
    return lax.psum_scatter(part, "row", scatter_dimension=0, tiled=True).astype(jnp.bfloat16)


MESH = pl.DeviceIdType.MESH
BF16, F32 = jnp.bfloat16, jnp.float32
UP, DOWN = 1024, 512
LAG_X, LAG_M, LAG_Z = 2, 4, 6


def gelu(v):
    return 0.5 * v * (1.0 + lax.erf(v * 0.7071067811865476))


def kernel(
    block,
    tokens, w_up, w_down, up_mask, down_mask,
    out,
    mask_up, mask_down, w, xb, acc, other, hid, own, to_x, from_x, to_z, from_z, final,
    mask_sem, load_sem, w_sem, own_send, fwd_send, x_recv, pre_send, pre_recv, hid_send, hid_recv,
    rx_send, rx_recv, rz_send, rz_recv, out_send, out_recv,
):
    row, core = lax.axis_index("row"), lax.axis_index("col")
    z, x = row // 2, row % 2
    count, feats = tokens.shape
    depth, hidden = w.shape
    ups, downs = hidden // UP, hidden // DOWN
    few = count // 8
    piece = count // 2
    pair = z // 2
    partner = z + 1 - 2 * (z % 2)
    near = pair == core
    far_end = jnp.logical_not(near) & ((z == 0) | (z == 3))
    far_mid = jnp.logical_not(near) & ((z == 1) | (z == 2))
    near_mid = near & ((z == 1) | (z == 2))
    onward = 3 - jnp.where(z >= 2, 2, 1)
    first = jnp.where(near, z % 2, 1 - core)
    second = 1 - first

    def loop(steps, body):
        lax.fori_loop(0, steps, lambda i, _: (body(i), 0)[1], 0)

    def span(start, size):
        return pl.ds(pl.multiple_of(start * size, size), size)

    def at(zz, xx, cc):
        return {"row": zz * 2 + xx, "col": cc}

    barrier = pltpu.get_barrier_semaphore()

    def greet(device):
        pl.semaphore_signal(barrier, inc=1, device_id=device, device_id_type=MESH)

    def reach(dz):
        return (z + dz >= 0) & (z + dz <= 3)

    for dz in (1, -1):

        @pl.when(reach(dz))
        def _():
            greet(at(z + dz, x, 0))
            greet(at(z + dz, x, 1))

    greet(at(z, 1 - x, 0))
    greet(at(z, 1 - x, 1))
    greet(at(z, x, 1 - core))

    def load_w(source, zl, n):
        place = (span(zl, depth // 2), span(n, UP))
        return pltpu.make_async_copy(source.at[place], w.at[place], w_sem.at[zl, n])

    def slot(zl, xs, h, q):
        rows = pl.ds(pl.multiple_of(h * count + q * piece, piece), piece)
        return xb.at[zl, rows, span(xs, feats)]

    masks = (
        pltpu.make_async_copy(up_mask, mask_up, mask_sem.at[0]),
        pltpu.make_async_copy(down_mask, mask_down, mask_sem.at[1]),
    )
    for copy in masks:
        copy.start()
    load = pltpu.make_async_copy(
        tokens, xb.at[z % 2, span(core, count), span(x, feats)], load_sem
    )
    pl.when(near)(lambda: load.start())
    loop(ups, lambda n: load_w(w_up, first, n).start())
    loop(ups, lambda n: load_w(w_up, second, n).start())
    sides = jnp.where((z == 0) | (z == 3), 2, 4)
    pl.semaphore_wait(barrier, 3 + sides)

    def send_own(kind, q, device):
        return pltpu.make_async_remote_copy(
            src_ref=tokens.at[pl.ds(q * piece, piece)],
            dst_ref=slot(z % 2, x, core, q),
            send_sem=own_send.at[kind, q], recv_sem=x_recv.at[z % 2, x, core, q],
            device_id=device, device_id_type=MESH,
        )

    def each_own(act):
        for q in (0, 1):
            pl.when(jnp.logical_not(near))(lambda: act(send_own(0, q, at(z, x, pair))))
            act(send_own(1, q, at(z, 1 - x, pair)))
            for kind, dz in ((2, 1), (3, -1)):
                pl.when(reach(dz))(lambda: act(send_own(kind, q, at(z + dz, x, pair))))

    each_own(lambda copy: copy.start())

    def copy_x(kind, zl, xs, h, q, device):
        return pltpu.make_async_remote_copy(
            src_ref=slot(zl, xs, h, q), dst_ref=slot(zl, xs, h, q),
            send_sem=fwd_send.at[kind, zl, h, q], recv_sem=x_recv.at[zl, xs, h, q],
            device_id=device, device_id_type=MESH,
        )

    across, mate = at(z, 1 - x, core), at(z, x, 1 - core)
    end = jnp.where(z >= 2, 3, 0)

    def got(zl, xs, h, q):
        copy_x(0, zl, xs, h, q, across).wait_recv()

    def near_across(q, h):
        got(first, 1 - x, h, q)
        if q == 1:
            copy_x(1, first, 1 - x, h, q, at(partner, x, core)).start()

    def near_along(q, h):
        got(second, x, h, q)
        pl.when(near_mid)(lambda: copy_x(2, second, x, h, q, at(onward, x, core)).start())
        if q == 0:
            copy_x(0, second, x, h, q, across).start()

    def far_first(q, h):
        got(first, x, h, q)
        pl.when(far_mid)(lambda: copy_x(1, first, x, h, q, at(end, x, core)).start())
        copy_x(0, first, x, h, q, across).start()

    def far_second(q, h):
        got(second, x, h, q)
        pl.when(far_mid)(lambda: copy_x(1, second, x, h, q, at(end, x, core)).start())
        copy_x(0, second, x, h, q, across).start()

    order = ((0, 0), (0, 1), (1, 0), (1, 1))

    @pl.when(near)
    def _():
        for q, h in order:
            near_across(q, h)
            near_along(q, h)
        load.wait()
        for q in (0, 1):
            got(first, x, 1 - core, q)

    @pl.when(jnp.logical_not(near))
    def _():
        for q, h in order:
            far_first(q, h)

    @pl.when(far_mid)
    def _():
        for q, h in order:
            far_second(q, h)

    @pl.when(jnp.logical_not(near))
    def _():
        for q, h in order:
            got(first, 1 - x, h, q)

    def masked(mask, row_at, rows, col_at, wide, mask_row, mask_col):
        parts = []
        for j in range(rows // block):
            place = pl.ds(pl.multiple_of(row_at + j * block, block), block)
            tiles = []
            for t in range(wide // block):
                cols = pl.ds(pl.multiple_of(col_at + t * block, block), block)
                keep = mask[mask_row + j, mask_col + t].astype(F32)
                tiles.append(w[place, cols] * jnp.full((block, block), keep, F32).astype(BF16))
            parts.append(jnp.concatenate(tiles, axis=1))
        return jnp.concatenate(parts, axis=0)

    def up_dot(n, start, rows, xs):
        kept = masked(
            mask_up, start, rows, n * UP, UP, (core * depth + start) // block, n * (UP // block)
        )
        return lax.dot_general(kept, xs, (((0,), (1,)), ((), ())), preferred_element_type=F32)

    def up_first(n):
        load_w(w_up, first, n).wait()
        acc[n] = up_dot(n, first * (depth // 2), depth // 2, xb[first])
        load_w(w_down, first, n).start()

    def up_more(n, xs):
        start = second * (depth // 2) + xs * feats
        acc[n] = acc[n] + up_dot(n, start, feats, xb[second, :, span(xs, feats)])

    def with_forward(n):
        up_first(n)
        for i, (q, h) in enumerate(order):
            pl.when(far_end & (n == i))(lambda: far_second(q, h))

    for copy in masks:
        copy.wait()
    loop(ups, with_forward)

    def up_second(n):
        load_w(w_up, second, n).wait()
        up_more(n, x)

    loop(ups, up_second)
    for q, h in order:
        got(second, 1 - x, h, q)

    def half(which):
        return span(which, count)

    def copy_pre(n):
        return pltpu.make_async_remote_copy(
            src_ref=acc.at[n, :, half(1 - core)], dst_ref=other.at[n],
            send_sem=pre_send.at[n], recv_sem=pre_recv.at[n],
            device_id=mate, device_id_type=MESH,
        )

    def copy_hid(n, which):
        return pltpu.make_async_remote_copy(
            src_ref=hid.at[span(n, UP), half(which)], dst_ref=hid.at[span(n, UP), half(which)],
            send_sem=hid_send.at[n], recv_sem=hid_recv.at[n],
            device_id=mate, device_id_type=MESH,
        )

    def up_last(n):
        up_more(n, 1 - x)
        copy_pre(n).start()
        load_w(w_down, second, n).start()

    def finish(n):
        copy_pre(n).wait_recv()
        hid[span(n, UP), half(core)] = gelu(acc[n, :, half(core)] + other[n]).astype(BF16)
        copy_hid(n, core).start()

    def middle(i):
        pl.when(i < ups)(lambda: up_last(i))
        pl.when(i >= 2)(lambda: finish(i - 2))

    loop(ups + 2, middle)
    loop(ups, lambda n: copy_hid(n, 1 - core).wait_recv())

    def copy_rx(n):
        return pltpu.make_async_remote_copy(
            src_ref=to_x.at[n], dst_ref=from_x.at[n],
            send_sem=rx_send.at[n], recv_sem=rx_recv.at[n],
            device_id=across, device_id_type=MESH,
        )

    MERGE = 4

    def copy_rz(n, dest, via, into):
        return pltpu.make_async_remote_copy(
            src_ref=to_z.at[n, dest], dst_ref=from_z.at[n, into],
            send_sem=rz_send.at[n, dest], recv_sem=rz_recv.at[n, into],
            device_id=at(via, x, core), device_id_type=MESH,
        )

    steps = ((0, 1), (1, -1), (2, 2), (3, -2))
    far_dest = 3 - end
    merges = (z == 1) | (z == 2)

    def down(n):
        for zl in (0, 1):
            pl.when(n % (UP // DOWN) == 0)(lambda: load_w(w_down, zl, n // (UP // DOWN)).wait())
        kept = masked(
            mask_down, 0, depth, n * DOWN, DOWN, 0, (core * downs + n) * (DOWN // block)
        )
        part = lax.dot_general(
            kept, hid[...], (((0,), (0,)), ((), ())), preferred_element_type=F32
        ).T.reshape(2, 4, 2, few, DOWN)
        for cp in range(2):
            for zp in range(4):
                pair_of = part[cp, zp]
                to_x[n, zp, cp] = jnp.where(x == 0, pair_of[1], pair_of[0]).astype(BF16)
                own[n, zp, cp] = jnp.where(x == 0, pair_of[0], pair_of[1])
        copy_rx(n).start()

    def each_rz(n, act):
        for into, dz in steps:
            if abs(dz) == 1:
                pl.when(reach(dz))(lambda: act(copy_rz(n, z + dz, z + dz, into)))
            else:
                pl.when(reach(dz) & jnp.logical_not(merges))(
                    lambda: act(copy_rz(n, z + dz, z + dz, into))
                )
        pl.when(jnp.logical_not(merges))(
            lambda: act(copy_rz(n, far_dest, partner, MERGE))
        )

    def merged_rz(n):
        into = jnp.where(z == 1, 2, 3)
        dest = jnp.where(z == 1, 3, 0)
        return copy_rz(n, dest, dest, into)

    def take_x(n):
        copy_rx(n).wait_recv()
        total = own[n] + from_x[n].astype(F32)
        own[n] = total
        to_z[n] = total.astype(BF16)
        each_rz(n, lambda copy: copy.start())

    def merge(n):
        @pl.when(merges)
        def _():
            copy_rz(n, z, z, MERGE).wait_recv()
            dest = jnp.where(z == 1, 3, 0)
            to_z[n, dest] = (own[n, dest] + from_z[n, MERGE].astype(F32)).astype(BF16)
            merged_rz(n).start()

    def copy_out(n):
        place = span(core * downs + n, DOWN)
        return pltpu.make_async_remote_copy(
            src_ref=final.at[:, span(n, DOWN)], dst_ref=out.at[:, place],
            send_sem=out_send.at[n], recv_sem=out_recv.at[n],
            device_id=mate, device_id_type=MESH,
        )

    def finish_out(n):
        for into, dz in steps:

            @pl.when(reach(-dz))
            def _():
                copy_rz(n, z, z, into).wait_recv()
                own[n, z] = own[n, z] + from_z[n, into].astype(F32)

        final[:, span(n, DOWN)] = own[n, z, 1 - core].astype(BF16)
        out[:, span(core * downs + n, DOWN)] = own[n, z, core].astype(BF16)
        copy_out(n).start()

    def pipeline(i):
        for n, stage in (
            (i, down), (i - LAG_X, take_x), (i - LAG_M, merge), (i - LAG_Z, finish_out),
        ):
            pl.when((n >= 0) & (n < downs))(functools.partial(stage, n))

    loop(downs + LAG_Z, pipeline)

    each_own(lambda copy: copy.wait_send())
    for q, h in order:

        @pl.when(near)
        def _():
            if q == 1:
                copy_x(1, first, 1 - x, h, q, at(partner, x, core)).wait_send()
            else:
                copy_x(0, second, x, h, q, across).wait_send()
            pl.when(near_mid)(lambda: copy_x(2, second, x, h, q, at(onward, x, core)).wait_send())

        @pl.when(jnp.logical_not(near))
        def _():
            copy_x(0, first, x, h, q, across).wait_send()
            copy_x(0, second, x, h, q, across).wait_send()
            pl.when(far_mid)(lambda: copy_x(1, first, x, h, q, at(end, x, core)).wait_send())
            pl.when(far_mid)(lambda: copy_x(1, second, x, h, q, at(end, x, core)).wait_send())

    def sent_up(n):
        copy_pre(n).wait_send()
        copy_hid(n, core).wait_send()

    loop(ups, sent_up)

    def sent_down(n):
        copy_rx(n).wait_send()
        each_rz(n, lambda copy: copy.wait_send())
        pl.when(merges)(lambda: merged_rz(n).wait_send())
        copy_out(n).wait()

    loop(downs, sent_down)


def fused(tokens, w_up, w_down, mask_up, mask_down):
    block = w_up.shape[0] * 2 // mask_up.shape[0]
    count, feats = tokens.shape
    depth, hidden = w_up.shape
    ups, downs = hidden // UP, hidden // DOWN
    few = count // 8
    dma = pltpu.SemaphoreType.DMA
    vmem = pl.BlockSpec(memory_space=pltpu.VMEM)
    hbm = pl.BlockSpec(memory_space=pl.ANY)
    travel = (downs, 4, 2, few, DOWN)
    return pl.pallas_call(
        functools.partial(kernel, block),
        out_shape=jax.ShapeDtypeStruct((few, w_down.shape[1] * 2), BF16),
        in_specs=[hbm] * 5,
        out_specs=vmem,
        scratch_shapes=[
            pltpu.SMEM(mask_up.shape, mask_up.dtype),
            pltpu.SMEM(mask_down.shape, mask_down.dtype),
            pltpu.VMEM((depth, hidden), BF16),
            pltpu.VMEM((2, 2 * count, 2 * feats), BF16),
            pltpu.VMEM((ups, UP, 2 * count), F32),
            pltpu.VMEM((ups, UP, count), F32),
            pltpu.VMEM((hidden, 2 * count), BF16),
            pltpu.VMEM(travel, F32),
            pltpu.VMEM(travel, BF16),
            pltpu.VMEM(travel, BF16),
            pltpu.VMEM(travel, BF16),
            pltpu.VMEM((downs, 5, 2, few, DOWN), BF16),
            pltpu.VMEM((few, w_down.shape[1]), BF16),
            dma((2,)),
            dma,
            dma((2, ups)),
            dma((6, 2)),
            dma((3, 2, 2, 2)),
            dma((2, 2, 2, 2)),
            dma((ups,)), dma((ups,)),
            dma((ups,)), dma((ups,)),
            dma((downs,)), dma((downs,)),
            dma((downs, 4)), dma((downs, 5)),
            dma((downs,)), dma((downs,)),
        ],
        compiler_params=pltpu.CompilerParams(
            collective_id=0, has_side_effects=True, vmem_limit_bytes=63 * 2**20
        ),
    )(tokens, w_up, w_down, mask_up, mask_down)


def per_device(tokens, w_up, w_down, mask_up, mask_down):
    sizes = (lax.axis_size("row"), lax.axis_size("col"))
    square = tokens.shape[1] * 4 == w_up.shape[0] == w_up.shape[1] == w_down.shape[0] == w_down.shape[1]
    if sizes == (8, 2) and square and tokens.shape[0] % 128 == 0 and w_up.shape[1] % UP == 0:
        return fused(tokens, w_up, w_down, mask_up, mask_down)
    return general(tokens, w_up, w_down, mask_up, mask_down)


def solution(mesh):
    return jax.shard_map(
        per_device,
        mesh=mesh,
        in_specs=(
            P(("groups", "col"), "row"),
            P("col", "row"),
            P("row", "col"),
            P(None, "row"),
            P("row", None),
        ),
        out_specs=P(("groups", "col", "row"), None),
        check_vma=False,
    )
```

```python
import functools

import jax
import jax.numpy as jnp
from jax import lax
from jax.experimental import pallas as pl
from jax.experimental.pallas import tpu as pltpu
from jax.sharding import PartitionSpec as P


def expand_mask(mask, block, dtype):
    count_r, count_c = mask.shape
    wide = jnp.broadcast_to(mask.astype(dtype)[:, None, :, None], (count_r, block, count_c, block))
    return wide.reshape(count_r * block, count_c * block)


def general(tokens, w_up, w_down, mask_up, mask_down):
    cols = lax.axis_size("col")
    block = w_up.shape[0] * cols // mask_up.shape[0]
    core = lax.axis_index("col")
    mine = lax.all_gather(tokens, "row", axis=1, tiled=True)
    x = lax.all_to_all(mine, "col", split_axis=1, concat_axis=0, tiled=True)
    half = mask_up.shape[0] // cols
    mask_u = lax.dynamic_slice_in_dim(mask_up, core * half, half, 0)
    pre = jnp.dot(
        x, w_up * expand_mask(mask_u, block, w_up.dtype), preferred_element_type=jnp.float32
    )
    swap = [(i, (i + 1) % cols) for i in range(cols)]
    pre = pre + lax.ppermute(pre.astype(jnp.bfloat16), "col", swap).astype(jnp.float32)
    hidden = jax.nn.gelu(pre, approximate=False).astype(jnp.bfloat16)
    half_d = mask_down.shape[1] // cols
    mask_d = lax.dynamic_slice_in_dim(mask_down, core * half_d, half_d, 1)
    part = jnp.dot(
        hidden,
        w_down * expand_mask(mask_d, block, w_down.dtype),
        preferred_element_type=jnp.float32,
    )
    part = lax.all_to_all(
        part.astype(jnp.bfloat16), "col", split_axis=0, concat_axis=1, tiled=True
    )
    return lax.psum_scatter(part, "row", scatter_dimension=0, tiled=True).astype(jnp.bfloat16)


MESH = pl.DeviceIdType.MESH
BF16, F32 = jnp.bfloat16, jnp.float32
UP, DOWN = 1024, 512
SEND = 256
SUBS = DOWN // SEND
LAG_X, LAG_Z = 3, 7
STEPS = (1, -1, 2, -2, 3, -3)


def gelu(v):
    return 0.5 * v * (1.0 + lax.erf(v * 0.7071067811865476))


def kernel(
    block,
    tokens, w_up, w_down, up_mask, down_mask,
    out,
    mask_up, mask_down, w, xb, acc, other, hid, own, to_x, from_x, to_z, from_z, final,
    mask_sem, load_sem, w_sem, own_send, fwd_send, x_recv, pre_send, pre_recv, hid_send, hid_recv,
    rx_send, rx_recv, rz_send, rz_recv, out_send, out_recv,
):
    row, core = lax.axis_index("row"), lax.axis_index("col")
    z, x = row // 2, row % 2
    count, feats = tokens.shape
    depth, hidden = w.shape
    ups, downs = hidden // UP, hidden // DOWN
    subs = hidden // SEND
    few = count // 8
    piece = count // 2
    pair = z // 2
    partner = z + 1 - 2 * (z % 2)
    near = pair == core
    far_end = jnp.logical_not(near) & ((z == 0) | (z == 3))
    far_mid = jnp.logical_not(near) & ((z == 1) | (z == 2))
    near_mid = near & ((z == 1) | (z == 2))
    onward = 3 - jnp.where(z >= 2, 2, 1)
    first = jnp.where(near, z % 2, 1 - core)
    second = 1 - first

    def loop(steps, body):
        lax.fori_loop(0, steps, lambda i, _: (body(i), 0)[1], 0)

    def span(start, size):
        return pl.ds(pl.multiple_of(start * size, size), size)

    def at(zz, xx, cc):
        return {"row": zz * 2 + xx, "col": cc}

    barrier = pltpu.get_barrier_semaphore()

    def greet(device):
        pl.semaphore_signal(barrier, inc=1, device_id=device, device_id_type=MESH)

    def reach(dz):
        return (z + dz >= 0) & (z + dz <= 3)

    for dz in (1, -1):

        @pl.when(reach(dz))
        def _():
            greet(at(z + dz, x, 0))
            greet(at(z + dz, x, 1))

    greet(at(z, 1 - x, 0))
    greet(at(z, 1 - x, 1))
    greet(at(z, x, 1 - core))

    def load_w(source, zl, n):
        place = (span(zl, depth // 2), span(n, UP))
        return pltpu.make_async_copy(source.at[place], w.at[place], w_sem.at[zl, n])

    def slot(zl, xs, h, q):
        rows = pl.ds(pl.multiple_of(h * count + q * piece, piece), piece)
        return xb.at[zl, rows, span(xs, feats)]

    masks = (
        pltpu.make_async_copy(up_mask, mask_up, mask_sem.at[0]),
        pltpu.make_async_copy(down_mask, mask_down, mask_sem.at[1]),
    )
    for copy in masks:
        copy.start()
    load = pltpu.make_async_copy(
        tokens, xb.at[z % 2, span(core, count), span(x, feats)], load_sem
    )
    pl.when(near)(lambda: load.start())
    loop(ups, lambda n: load_w(w_up, first, n).start())
    loop(ups, lambda n: load_w(w_up, second, n).start())
    sides = jnp.where((z == 0) | (z == 3), 2, 4)
    pl.semaphore_wait(barrier, 3 + sides)

    def send_own(kind, q, device):
        return pltpu.make_async_remote_copy(
            src_ref=tokens.at[pl.ds(q * piece, piece)],
            dst_ref=slot(z % 2, x, core, q),
            send_sem=own_send.at[kind, q], recv_sem=x_recv.at[z % 2, x, core, q],
            device_id=device, device_id_type=MESH,
        )

    def each_own(act):
        for q in (0, 1):
            pl.when(jnp.logical_not(near))(lambda: act(send_own(0, q, at(z, x, pair))))
            act(send_own(1, q, at(z, 1 - x, pair)))
            for kind, dz in ((2, 1), (3, -1)):
                pl.when(reach(dz))(lambda: act(send_own(kind, q, at(z + dz, x, pair))))

    each_own(lambda copy: copy.start())

    def copy_x(kind, zl, xs, h, q, device):
        return pltpu.make_async_remote_copy(
            src_ref=slot(zl, xs, h, q), dst_ref=slot(zl, xs, h, q),
            send_sem=fwd_send.at[kind, zl, h, q], recv_sem=x_recv.at[zl, xs, h, q],
            device_id=device, device_id_type=MESH,
        )

    across, mate = at(z, 1 - x, core), at(z, x, 1 - core)
    end = jnp.where(z >= 2, 3, 0)

    def got(zl, xs, h, q):
        copy_x(0, zl, xs, h, q, across).wait_recv()

    def near_across(q, h):
        got(first, 1 - x, h, q)

    def near_along(q, h):
        got(second, x, h, q)
        pl.when(near_mid)(lambda: copy_x(2, second, x, h, q, at(onward, x, core)).start())
        if q == 0:
            copy_x(0, second, x, h, q, across).start()

    def far_first(q, h):
        got(first, x, h, q)
        pl.when(far_mid)(lambda: copy_x(1, first, x, h, q, at(end, x, core)).start())
        copy_x(0, first, x, h, q, across).start()

    def far_second(q, h):
        got(second, x, h, q)
        pl.when(far_mid)(lambda: copy_x(1, second, x, h, q, at(end, x, core)).start())
        copy_x(0, second, x, h, q, across).start()

    order = ((0, 0), (0, 1), (1, 0), (1, 1))

    @pl.when(near)
    def _():
        for q, h in order:
            near_across(q, h)
            near_along(q, h)
        load.wait()
        for q in (0, 1):
            got(first, x, 1 - core, q)

    @pl.when(jnp.logical_not(near))
    def _():
        for q, h in order:
            far_first(q, h)

    @pl.when(far_mid)
    def _():
        for q, h in order:
            far_second(q, h)

    @pl.when(jnp.logical_not(near))
    def _():
        for q, h in order:
            got(first, 1 - x, h, q)

    def masked(mask, row_at, rows, col_at, wide, mask_row, mask_col):
        parts = []
        for j in range(rows // block):
            place = pl.ds(pl.multiple_of(row_at + j * block, block), block)
            tiles = []
            for t in range(wide // block):
                cols = pl.ds(pl.multiple_of(col_at + t * block, block), block)
                keep = mask[mask_row + j, mask_col + t].astype(F32)
                tiles.append(w[place, cols] * jnp.full((block, block), keep, F32).astype(BF16))
            parts.append(jnp.concatenate(tiles, axis=1))
        return jnp.concatenate(parts, axis=0)

    def up_dot(n, start, rows, xs):
        kept = masked(
            mask_up, start, rows, n * UP, UP, (core * depth + start) // block, n * (UP // block)
        )
        return lax.dot_general(kept, xs, (((0,), (1,)), ((), ())), preferred_element_type=F32)

    def up_first(n):
        load_w(w_up, first, n).wait()
        acc[n] = up_dot(n, first * (depth // 2), depth // 2, xb[first])
        load_w(w_down, first, n).start()

    def up_more(n, xs):
        start = second * (depth // 2) + xs * feats
        acc[n] = acc[n] + up_dot(n, start, feats, xb[second, :, span(xs, feats)])

    def with_forward(n):
        up_first(n)
        for i, (q, h) in enumerate(order):
            pl.when(far_end & (n == i))(lambda: far_second(q, h))

    for copy in masks:
        copy.wait()
    loop(ups, with_forward)
    for h in (0, 1):
        pl.when(near)(lambda: copy_x(1, first, 1 - x, h, 1, at(partner, x, core)).start())

    def up_second(n):
        load_w(w_up, second, n).wait()
        up_more(n, x)

    loop(ups, up_second)
    for q, h in order:
        got(second, 1 - x, h, q)

    def half(which):
        return span(which, count)

    def copy_pre(n):
        return pltpu.make_async_remote_copy(
            src_ref=acc.at[n, :, half(1 - core)], dst_ref=other.at[n],
            send_sem=pre_send.at[n], recv_sem=pre_recv.at[n],
            device_id=mate, device_id_type=MESH,
        )

    def copy_hid(n, which):
        return pltpu.make_async_remote_copy(
            src_ref=hid.at[span(n, UP), half(which)], dst_ref=hid.at[span(n, UP), half(which)],
            send_sem=hid_send.at[n], recv_sem=hid_recv.at[n],
            device_id=mate, device_id_type=MESH,
        )

    def up_last(n):
        up_more(n, 1 - x)
        copy_pre(n).start()
        load_w(w_down, second, n).start()

    def finish(n):
        copy_pre(n).wait_recv()
        hid[span(n, UP), half(core)] = gelu(acc[n, :, half(core)] + other[n]).astype(BF16)
        copy_hid(n, core).start()

    loop(ups, up_last)
    loop(ups, finish)
    loop(ups, lambda n: copy_hid(n, 1 - core).wait_recv())

    def copy_rx(n):
        return pltpu.make_async_remote_copy(
            src_ref=to_x.at[n], dst_ref=from_x.at[n],
            send_sem=rx_send.at[n], recv_sem=rx_recv.at[n],
            device_id=across, device_id_type=MESH,
        )

    def copy_rz(n, i):
        dz = STEPS[i]
        return pltpu.make_async_remote_copy(
            src_ref=to_z.at[n, jnp.clip(z + dz, 0, 3)], dst_ref=from_z.at[n, i],
            send_sem=rz_send.at[n, i], recv_sem=rz_recv.at[n, i],
            device_id=at(z + dz, x, core), device_id_type=MESH,
        )

    def each_rz(n, act):
        for i, dz in enumerate(STEPS):
            pl.when(reach(dz))(lambda: act(copy_rz(n, i)))

    def down(n):
        for zl in (0, 1):
            pl.when(n % (UP // DOWN) == 0)(lambda: load_w(w_down, zl, n // (UP // DOWN)).wait())
        kept = masked(
            mask_down, 0, depth, n * DOWN, DOWN, 0, (core * downs + n) * (DOWN // block)
        )
        part = lax.dot_general(
            kept, hid[...], (((0,), (0,)), ((), ())), preferred_element_type=F32
        ).T.reshape(2, 4, 2, few, DOWN)
        for s in range(SUBS):
            cols = slice(s * SEND, (s + 1) * SEND)
            for cp in range(2):
                for zp in range(4):
                    both = part[cp, zp, :, :, cols]
                    to_x[n * SUBS + s, zp, cp] = jnp.where(x == 0, both[1], both[0]).astype(BF16)
                    own[n * SUBS + s, zp, cp] = jnp.where(x == 0, both[0], both[1])
            copy_rx(n * SUBS + s).start()

    def take_x(n):
        copy_rx(n).wait_recv()
        total = own[n] + from_x[n].astype(F32)
        own[n] = total
        to_z[n] = total.astype(BF16)
        each_rz(n, lambda copy: copy.start())

    def copy_out(n):
        place = span(core * subs + n, SEND)
        return pltpu.make_async_remote_copy(
            src_ref=final.at[:, span(n, SEND)], dst_ref=out.at[:, place],
            send_sem=out_send.at[n], recv_sem=out_recv.at[n],
            device_id=mate, device_id_type=MESH,
        )

    def finish_out(n):
        for i, dz in enumerate(STEPS):

            @pl.when(reach(-dz))
            def _():
                copy_rz(n, i).wait_recv()
                own[n, z] = own[n, z] + from_z[n, i].astype(F32)

        final[:, span(n, SEND)] = own[n, z, 1 - core].astype(BF16)
        copy_out(n).start()
        out[:, span(core * subs + n, SEND)] = own[n, z, core].astype(BF16)

    def pipeline(i):
        pl.when((i % SUBS == 0) & (i < subs))(lambda: down(i // SUBS))
        for n, stage in ((i - LAG_X, take_x), (i - LAG_Z, finish_out)):
            pl.when((n >= 0) & (n < subs))(functools.partial(stage, n))

    loop(subs + LAG_Z, pipeline)

    each_own(lambda copy: copy.wait_send())
    for q, h in order:

        @pl.when(near)
        def _():
            if q == 1:
                copy_x(1, first, 1 - x, h, q, at(partner, x, core)).wait_send()
            else:
                copy_x(0, second, x, h, q, across).wait_send()
            pl.when(near_mid)(lambda: copy_x(2, second, x, h, q, at(onward, x, core)).wait_send())

        @pl.when(jnp.logical_not(near))
        def _():
            copy_x(0, first, x, h, q, across).wait_send()
            copy_x(0, second, x, h, q, across).wait_send()
            pl.when(far_mid)(lambda: copy_x(1, first, x, h, q, at(end, x, core)).wait_send())
            pl.when(far_mid)(lambda: copy_x(1, second, x, h, q, at(end, x, core)).wait_send())

    def sent_up(n):
        copy_pre(n).wait_send()
        copy_hid(n, core).wait_send()

    loop(ups, sent_up)

    def sent_down(n):
        copy_rx(n).wait_send()
        each_rz(n, lambda copy: copy.wait_send())
        copy_out(n).wait()

    loop(subs, sent_down)


def fused(tokens, w_up, w_down, mask_up, mask_down):
    block = w_up.shape[0] * 2 // mask_up.shape[0]
    count, feats = tokens.shape
    depth, hidden = w_up.shape
    ups, downs = hidden // UP, hidden // DOWN
    few = count // 8
    dma = pltpu.SemaphoreType.DMA
    vmem = pl.BlockSpec(memory_space=pltpu.VMEM)
    hbm = pl.BlockSpec(memory_space=pl.ANY)
    subs = hidden // SEND
    travel = (subs, 4, 2, few, SEND)
    return pl.pallas_call(
        functools.partial(kernel, block),
        out_shape=jax.ShapeDtypeStruct((few, w_down.shape[1] * 2), BF16),
        in_specs=[hbm] * 5,
        out_specs=vmem,
        scratch_shapes=[
            pltpu.SMEM(mask_up.shape, mask_up.dtype),
            pltpu.SMEM(mask_down.shape, mask_down.dtype),
            pltpu.VMEM((depth, hidden), BF16),
            pltpu.VMEM((2, 2 * count, 2 * feats), BF16),
            pltpu.VMEM((ups, UP, 2 * count), F32),
            pltpu.VMEM((ups, UP, count), F32),
            pltpu.VMEM((hidden, 2 * count), BF16),
            pltpu.VMEM(travel, F32),
            pltpu.VMEM(travel, BF16),
            pltpu.VMEM(travel, BF16),
            pltpu.VMEM(travel, BF16),
            pltpu.VMEM((subs, len(STEPS), 2, few, SEND), BF16),
            pltpu.VMEM((few, w_down.shape[1]), BF16),
            dma((2,)),
            dma,
            dma((2, ups)),
            dma((6, 2)),
            dma((3, 2, 2, 2)),
            dma((2, 2, 2, 2)),
            dma((ups,)), dma((ups,)),
            dma((ups,)), dma((ups,)),
            dma((subs,)), dma((subs,)),
            dma((subs, len(STEPS))), dma((subs, len(STEPS))),
            dma((subs,)), dma((subs,)),
        ],
        compiler_params=pltpu.CompilerParams(
            collective_id=0, has_side_effects=True, vmem_limit_bytes=63 * 2**20
        ),
    )(tokens, w_up, w_down, mask_up, mask_down)


def per_device(tokens, w_up, w_down, mask_up, mask_down):
    sizes = (lax.axis_size("row"), lax.axis_size("col"))
    square = tokens.shape[1] * 4 == w_up.shape[0] == w_up.shape[1] == w_down.shape[0] == w_down.shape[1]
    if sizes == (8, 2) and square and tokens.shape[0] % 128 == 0 and w_up.shape[1] % UP == 0:
        return fused(tokens, w_up, w_down, mask_up, mask_down)
    return general(tokens, w_up, w_down, mask_up, mask_down)


def solution(mesh):
    return jax.shard_map(
        per_device,
        mesh=mesh,
        in_specs=(
            P(("groups", "col"), "row"),
            P("col", "row"),
            P("row", "col"),
            P(None, "row"),
            P("row", None),
        ),
        out_specs=P(("groups", "col", "row"), None),
        check_vma=False,
    )
```

```python
import functools

import jax
import jax.numpy as jnp
from jax import lax
from jax.experimental import pallas as pl
from jax.experimental.pallas import tpu as pltpu
from jax.sharding import PartitionSpec as P


def expand_mask(mask, block, dtype):
    count_r, count_c = mask.shape
    wide = jnp.broadcast_to(mask.astype(dtype)[:, None, :, None], (count_r, block, count_c, block))
    return wide.reshape(count_r * block, count_c * block)


def general(tokens, w_up, w_down, mask_up, mask_down):
    cols = lax.axis_size("col")
    block = w_up.shape[0] * cols // mask_up.shape[0]
    core = lax.axis_index("col")
    mine = lax.all_gather(tokens, "row", axis=1, tiled=True)
    x = lax.all_to_all(mine, "col", split_axis=1, concat_axis=0, tiled=True)
    half = mask_up.shape[0] // cols
    mask_u = lax.dynamic_slice_in_dim(mask_up, core * half, half, 0)
    pre = jnp.dot(
        x, w_up * expand_mask(mask_u, block, w_up.dtype), preferred_element_type=jnp.float32
    )
    swap = [(i, (i + 1) % cols) for i in range(cols)]
    pre = pre + lax.ppermute(pre.astype(jnp.bfloat16), "col", swap).astype(jnp.float32)
    hidden = jax.nn.gelu(pre, approximate=False).astype(jnp.bfloat16)
    half_d = mask_down.shape[1] // cols
    mask_d = lax.dynamic_slice_in_dim(mask_down, core * half_d, half_d, 1)
    part = jnp.dot(
        hidden,
        w_down * expand_mask(mask_d, block, w_down.dtype),
        preferred_element_type=jnp.float32,
    )
    part = lax.all_to_all(
        part.astype(jnp.bfloat16), "col", split_axis=0, concat_axis=1, tiled=True
    )
    return lax.psum_scatter(part, "row", scatter_dimension=0, tiled=True).astype(jnp.bfloat16)


MESH = pl.DeviceIdType.MESH
BF16, F32 = jnp.bfloat16, jnp.float32
UP, DOWN = 1024, 512
SEND = 512
SUBS = DOWN // SEND
LAG_X, LAG_Z = 2, 5
STEPS = (1, -1, 2, -2, 3, -3)


def gelu(v):
    return 0.5 * v * (1.0 + lax.erf(v * 0.7071067811865476))


def kernel(
    block,
    tokens, w_up, w_down, up_mask, down_mask,
    out,
    mask_up, mask_down, w, xb, acc, other, hid, own, to_x, from_x, to_z, from_z, final,
    mask_sem, load_sem, w_sem, own_send, fwd_send, x_recv, pre_send, pre_recv, hid_send, hid_recv,
    rx_send, rx_recv, rz_send, rz_recv, out_send, out_recv,
):
    row, core = lax.axis_index("row"), lax.axis_index("col")
    z, x = row // 2, row % 2
    count, feats = tokens.shape
    depth, hidden = w.shape
    ups, downs = hidden // UP, hidden // DOWN
    subs = hidden // SEND
    few = count // 8
    piece = count // 2
    pair = z // 2
    partner = z + 1 - 2 * (z % 2)
    near = pair == core
    far_end = jnp.logical_not(near) & ((z == 0) | (z == 3))
    far_mid = jnp.logical_not(near) & ((z == 1) | (z == 2))
    near_mid = near & ((z == 1) | (z == 2))
    onward = 3 - jnp.where(z >= 2, 2, 1)
    first = jnp.where(near, z % 2, 1 - core)
    second = 1 - first

    def loop(steps, body):
        lax.fori_loop(0, steps, lambda i, _: (body(i), 0)[1], 0)

    def span(start, size):
        return pl.ds(pl.multiple_of(start * size, size), size)

    def at(zz, xx, cc):
        return {"row": zz * 2 + xx, "col": cc}

    barrier = pltpu.get_barrier_semaphore()

    def greet(device):
        pl.semaphore_signal(barrier, inc=1, device_id=device, device_id_type=MESH)

    def reach(dz):
        return (z + dz >= 0) & (z + dz <= 3)

    for dz in (1, -1):

        @pl.when(reach(dz))
        def _():
            greet(at(z + dz, x, 0))
            greet(at(z + dz, x, 1))

    greet(at(z, 1 - x, 0))
    greet(at(z, 1 - x, 1))
    greet(at(z, x, 1 - core))

    def load_w(source, zl, n):
        place = (span(zl, depth // 2), span(n, UP))
        return pltpu.make_async_copy(source.at[place], w.at[place], w_sem.at[zl, n])

    def slot(zl, xs, h, q):
        rows = pl.ds(pl.multiple_of(h * count + q * piece, piece), piece)
        return xb.at[zl, rows, span(xs, feats)]

    masks = (
        pltpu.make_async_copy(up_mask, mask_up, mask_sem.at[0]),
        pltpu.make_async_copy(down_mask, mask_down, mask_sem.at[1]),
    )
    for copy in masks:
        copy.start()
    load = pltpu.make_async_copy(
        tokens, xb.at[z % 2, span(core, count), span(x, feats)], load_sem
    )
    pl.when(near)(lambda: load.start())
    loop(ups, lambda n: load_w(w_up, first, n).start())
    loop(ups, lambda n: load_w(w_up, second, n).start())
    sides = jnp.where((z == 0) | (z == 3), 2, 4)
    pl.semaphore_wait(barrier, 3 + sides)

    def send_own(kind, q, device):
        return pltpu.make_async_remote_copy(
            src_ref=tokens.at[pl.ds(q * piece, piece)],
            dst_ref=slot(z % 2, x, core, q),
            send_sem=own_send.at[kind, q], recv_sem=x_recv.at[z % 2, x, core, q],
            device_id=device, device_id_type=MESH,
        )

    def each_own(act):
        for q in (0, 1):
            pl.when(jnp.logical_not(near))(lambda: act(send_own(0, q, at(z, x, pair))))
            act(send_own(1, q, at(z, 1 - x, pair)))
            for kind, dz in ((2, 1), (3, -1)):
                pl.when(reach(dz))(lambda: act(send_own(kind, q, at(z + dz, x, pair))))

    each_own(lambda copy: copy.start())

    def copy_x(kind, zl, xs, h, q, device):
        return pltpu.make_async_remote_copy(
            src_ref=slot(zl, xs, h, q), dst_ref=slot(zl, xs, h, q),
            send_sem=fwd_send.at[kind, zl, h, q], recv_sem=x_recv.at[zl, xs, h, q],
            device_id=device, device_id_type=MESH,
        )

    across, mate = at(z, 1 - x, core), at(z, x, 1 - core)
    end = jnp.where(z >= 2, 3, 0)

    def got(zl, xs, h, q):
        copy_x(0, zl, xs, h, q, across).wait_recv()

    def near_along(q, h):
        got(second, x, h, q)
        pl.when(near_mid)(lambda: copy_x(2, second, x, h, q, at(onward, x, core)).start())
        if q == 0:
            copy_x(0, second, x, h, q, across).start()

    def far_first(q, h):
        got(first, x, h, q)
        pl.when(far_mid)(lambda: copy_x(1, first, x, h, q, at(end, x, core)).start())
        copy_x(0, first, x, h, q, across).start()

    def far_second(q, h):
        got(second, x, h, q)
        pl.when(far_mid)(lambda: copy_x(1, second, x, h, q, at(end, x, core)).start())
        copy_x(0, second, x, h, q, across).start()

    order = ((0, 0), (0, 1), (1, 0), (1, 1))

    def masked(mask, row_at, rows, col_at, wide, mask_row, mask_col):
        parts = []
        for j in range(rows // block):
            place = pl.ds(pl.multiple_of(row_at + j * block, block), block)
            tiles = []
            for t in range(wide // block):
                cols = pl.ds(pl.multiple_of(col_at + t * block, block), block)
                keep = mask[mask_row + j, mask_col + t].astype(F32)
                tiles.append(w[place, cols] * jnp.full((block, block), keep, F32).astype(BF16))
            parts.append(jnp.concatenate(tiles, axis=1))
        return jnp.concatenate(parts, axis=0)

    def up_dot(n, start, rows, xs):
        kept = masked(
            mask_up, start, rows, n * UP, UP, (core * depth + start) // block, n * (UP // block)
        )
        return lax.dot_general(kept, xs, (((0,), (1,)), ((), ())), preferred_element_type=F32)

    def up_start(n):
        load_w(w_up, first, n).wait()
        start = first * (depth // 2) + x * feats
        acc[n] = up_dot(n, start, feats, xb[first, :, span(x, feats)])

    def up_more(n, zl, xs):
        start = zl * (depth // 2) + xs * feats
        acc[n] = acc[n] + up_dot(n, start, feats, xb[zl, :, span(xs, feats)])

    for copy in masks:
        copy.wait()

    @pl.when(near)
    def _():
        load.wait()
        for q in (0, 1):
            got(first, x, 1 - core, q)

    @pl.when(jnp.logical_not(near))
    def _():
        for q, h in order:
            far_first(q, h)

    @pl.when(far_mid)
    def _():
        for q, h in order:
            far_second(q, h)

    def start_forward(n):
        up_start(n)
        for i, (q, h) in enumerate(order):
            pl.when(near & (n == i))(lambda: near_along(q, h))

    loop(ups, start_forward)
    for q, h in order:
        got(first, 1 - x, h, q)

    def with_forward(n):
        up_more(n, first, 1 - x)
        load_w(w_down, first, n).start()
        for i, (q, h) in enumerate(order):
            pl.when(far_end & (n == i))(lambda: far_second(q, h))

    loop(ups, with_forward)
    for h in (0, 1):
        pl.when(near)(lambda: copy_x(1, first, 1 - x, h, 1, at(partner, x, core)).start())

    def up_second(n):
        load_w(w_up, second, n).wait()
        up_more(n, second, x)

    loop(ups, up_second)
    for q, h in order:
        got(second, 1 - x, h, q)

    def half(which):
        return span(which, count)

    def copy_pre(n):
        return pltpu.make_async_remote_copy(
            src_ref=acc.at[n, :, half(1 - core)], dst_ref=other.at[n],
            send_sem=pre_send.at[n], recv_sem=pre_recv.at[n],
            device_id=mate, device_id_type=MESH,
        )

    def copy_hid(n, which):
        return pltpu.make_async_remote_copy(
            src_ref=hid.at[span(n, UP), half(which)], dst_ref=hid.at[span(n, UP), half(which)],
            send_sem=hid_send.at[n], recv_sem=hid_recv.at[n],
            device_id=mate, device_id_type=MESH,
        )

    def up_last(n):
        up_more(n, second, 1 - x)
        copy_pre(n).start()
        load_w(w_down, second, n).start()

    def finish(n):
        copy_pre(n).wait_recv()
        hid[span(n, UP), half(core)] = gelu(acc[n, :, half(core)] + other[n]).astype(BF16)
        copy_hid(n, core).start()

    loop(ups, up_last)
    loop(ups, finish)
    loop(ups, lambda n: copy_hid(n, 1 - core).wait_recv())

    def copy_rx(n):
        return pltpu.make_async_remote_copy(
            src_ref=to_x.at[n], dst_ref=from_x.at[n],
            send_sem=rx_send.at[n], recv_sem=rx_recv.at[n],
            device_id=across, device_id_type=MESH,
        )

    def copy_rz(n, i):
        dz = STEPS[i]
        return pltpu.make_async_remote_copy(
            src_ref=to_z.at[n, jnp.clip(z + dz, 0, 3)], dst_ref=from_z.at[n, i],
            send_sem=rz_send.at[n, i], recv_sem=rz_recv.at[n, i],
            device_id=at(z + dz, x, core), device_id_type=MESH,
        )

    def each_rz(n, act):
        for i, dz in enumerate(STEPS):
            pl.when(reach(dz))(lambda: act(copy_rz(n, i)))

    def down(n):
        for zl in (0, 1):
            pl.when(n % (UP // DOWN) == 0)(lambda: load_w(w_down, zl, n // (UP // DOWN)).wait())
        kept = masked(
            mask_down, 0, depth, n * DOWN, DOWN, 0, (core * downs + n) * (DOWN // block)
        )
        part = lax.dot_general(
            kept, hid[...], (((0,), (0,)), ((), ())), preferred_element_type=F32
        ).T.reshape(2, 4, 2, few, DOWN)
        for s in range(SUBS):
            cols = slice(s * SEND, (s + 1) * SEND)
            for cp in range(2):
                for zp in range(4):
                    both = part[cp, zp, :, :, cols]
                    to_x[n * SUBS + s, zp, cp] = jnp.where(x == 0, both[1], both[0]).astype(BF16)
                    own[n * SUBS + s, zp, cp] = jnp.where(x == 0, both[0], both[1])
            copy_rx(n * SUBS + s).start()

    def take_x(n):
        copy_rx(n).wait_recv()
        total = own[n] + from_x[n].astype(F32)
        own[n] = total
        to_z[n] = total.astype(BF16)
        each_rz(n, lambda copy: copy.start())

    def copy_out(n):
        place = span(core * subs + n, SEND)
        return pltpu.make_async_remote_copy(
            src_ref=final.at[:, span(n, SEND)], dst_ref=out.at[:, place],
            send_sem=out_send.at[n], recv_sem=out_recv.at[n],
            device_id=mate, device_id_type=MESH,
        )

    def finish_out(n):
        for i, dz in enumerate(STEPS):

            @pl.when(reach(-dz))
            def _():
                copy_rz(n, i).wait_recv()
                own[n, z] = own[n, z] + from_z[n, i].astype(F32)

        final[:, span(n, SEND)] = own[n, z, 1 - core].astype(BF16)
        copy_out(n).start()
        out[:, span(core * subs + n, SEND)] = own[n, z, core].astype(BF16)

    def pipeline(i):
        pl.when((i % SUBS == 0) & (i < subs))(lambda: down(i // SUBS))
        for n, stage in ((i - LAG_X, take_x), (i - LAG_Z, finish_out)):
            pl.when((n >= 0) & (n < subs))(functools.partial(stage, n))

    loop(subs + LAG_Z, pipeline)

    each_own(lambda copy: copy.wait_send())
    for q, h in order:

        @pl.when(near)
        def _():
            if q == 1:
                copy_x(1, first, 1 - x, h, q, at(partner, x, core)).wait_send()
            else:
                copy_x(0, second, x, h, q, across).wait_send()
            pl.when(near_mid)(lambda: copy_x(2, second, x, h, q, at(onward, x, core)).wait_send())

        @pl.when(jnp.logical_not(near))
        def _():
            copy_x(0, first, x, h, q, across).wait_send()
            copy_x(0, second, x, h, q, across).wait_send()
            pl.when(far_mid)(lambda: copy_x(1, first, x, h, q, at(end, x, core)).wait_send())
            pl.when(far_mid)(lambda: copy_x(1, second, x, h, q, at(end, x, core)).wait_send())

    def sent_up(n):
        copy_pre(n).wait_send()
        copy_hid(n, core).wait_send()

    loop(ups, sent_up)

    def sent_down(n):
        copy_rx(n).wait_send()
        each_rz(n, lambda copy: copy.wait_send())
        copy_out(n).wait()

    loop(subs, sent_down)


def fused(tokens, w_up, w_down, mask_up, mask_down):
    block = w_up.shape[0] * 2 // mask_up.shape[0]
    count, feats = tokens.shape
    depth, hidden = w_up.shape
    ups, downs = hidden // UP, hidden // DOWN
    few = count // 8
    dma = pltpu.SemaphoreType.DMA
    vmem = pl.BlockSpec(memory_space=pltpu.VMEM)
    hbm = pl.BlockSpec(memory_space=pl.ANY)
    subs = hidden // SEND
    travel = (subs, 4, 2, few, SEND)
    return pl.pallas_call(
        functools.partial(kernel, block),
        out_shape=jax.ShapeDtypeStruct((few, w_down.shape[1] * 2), BF16),
        in_specs=[hbm] * 5,
        out_specs=vmem,
        scratch_shapes=[
            pltpu.SMEM(mask_up.shape, mask_up.dtype),
            pltpu.SMEM(mask_down.shape, mask_down.dtype),
            pltpu.VMEM((depth, hidden), BF16),
            pltpu.VMEM((2, 2 * count, 2 * feats), BF16),
            pltpu.VMEM((ups, UP, 2 * count), F32),
            pltpu.VMEM((ups, UP, count), F32),
            pltpu.VMEM((hidden, 2 * count), BF16),
            pltpu.VMEM(travel, F32),
            pltpu.VMEM(travel, BF16),
            pltpu.VMEM(travel, BF16),
            pltpu.VMEM(travel, BF16),
            pltpu.VMEM((subs, len(STEPS), 2, few, SEND), BF16),
            pltpu.VMEM((few, w_down.shape[1]), BF16),
            dma((2,)),
            dma,
            dma((2, ups)),
            dma((6, 2)),
            dma((3, 2, 2, 2)),
            dma((2, 2, 2, 2)),
            dma((ups,)), dma((ups,)),
            dma((ups,)), dma((ups,)),
            dma((subs,)), dma((subs,)),
            dma((subs, len(STEPS))), dma((subs, len(STEPS))),
            dma((subs,)), dma((subs,)),
        ],
        compiler_params=pltpu.CompilerParams(
            collective_id=0, has_side_effects=True, vmem_limit_bytes=63 * 2**20
        ),
    )(tokens, w_up, w_down, mask_up, mask_down)


def per_device(tokens, w_up, w_down, mask_up, mask_down):
    sizes = (lax.axis_size("row"), lax.axis_size("col"))
    square = tokens.shape[1] * 4 == w_up.shape[0] == w_up.shape[1] == w_down.shape[0] == w_down.shape[1]
    if sizes == (8, 2) and square and tokens.shape[0] % 128 == 0 and w_up.shape[1] % UP == 0:
        return fused(tokens, w_up, w_down, mask_up, mask_down)
    return general(tokens, w_up, w_down, mask_up, mask_down)


def solution(mesh):
    return jax.shard_map(
        per_device,
        mesh=mesh,
        in_specs=(
            P(("groups", "col"), "row"),
            P("col", "row"),
            P("row", "col"),
            P(None, "row"),
            P("row", None),
        ),
        out_specs=P(("groups", "col", "row"), None),
        check_vma=False,
    )
```

```python
import functools

import jax
import jax.numpy as jnp
from jax import lax
from jax.experimental import pallas as pl
from jax.experimental.pallas import tpu as pltpu
from jax.sharding import PartitionSpec as P


def expand_mask(mask, block, dtype):
    count_r, count_c = mask.shape
    wide = jnp.broadcast_to(mask.astype(dtype)[:, None, :, None], (count_r, block, count_c, block))
    return wide.reshape(count_r * block, count_c * block)


def general(tokens, w_up, w_down, mask_up, mask_down):
    cols = lax.axis_size("col")
    block = w_up.shape[0] * cols // mask_up.shape[0]
    core = lax.axis_index("col")
    mine = lax.all_gather(tokens, "row", axis=1, tiled=True)
    x = lax.all_to_all(mine, "col", split_axis=1, concat_axis=0, tiled=True)
    half = mask_up.shape[0] // cols
    mask_u = lax.dynamic_slice_in_dim(mask_up, core * half, half, 0)
    pre = jnp.dot(
        x, w_up * expand_mask(mask_u, block, w_up.dtype), preferred_element_type=jnp.float32
    )
    swap = [(i, (i + 1) % cols) for i in range(cols)]
    pre = pre + lax.ppermute(pre.astype(jnp.bfloat16), "col", swap).astype(jnp.float32)
    hidden = jax.nn.gelu(pre, approximate=False).astype(jnp.bfloat16)
    half_d = mask_down.shape[1] // cols
    mask_d = lax.dynamic_slice_in_dim(mask_down, core * half_d, half_d, 1)
    part = jnp.dot(
        hidden,
        w_down * expand_mask(mask_d, block, w_down.dtype),
        preferred_element_type=jnp.float32,
    )
    part = lax.all_to_all(
        part.astype(jnp.bfloat16), "col", split_axis=0, concat_axis=1, tiled=True
    )
    return lax.psum_scatter(part, "row", scatter_dimension=0, tiled=True).astype(jnp.bfloat16)


MESH = pl.DeviceIdType.MESH
BF16, F32 = jnp.bfloat16, jnp.float32
UP, DOWN = 1024, 512
SEND = 512
SUBS = DOWN // SEND
LAG_X, LAG_Z = 2, 5
STEPS = (1, -1, 2, -2, 3, -3)


def gelu(v):
    return 0.5 * v * (1.0 + lax.erf(v * 0.7071067811865476))


def kernel(
    block,
    tokens, w_up, w_down, up_mask, down_mask,
    out,
    mask_up, mask_down, w, xb, acc, other, hid, own, to_x, from_x, to_z, from_z, final,
    mask_sem, load_sem, w_sem, own_send, fwd_send, x_recv, pre_send, pre_recv, hid_send, hid_recv,
    rx_send, rx_recv, rz_send, rz_recv, out_send, out_recv,
):
    row, core = lax.axis_index("row"), lax.axis_index("col")
    z, x = row // 2, row % 2
    count, feats = tokens.shape
    depth, hidden = w.shape
    ups, downs = hidden // UP, hidden // DOWN
    subs = hidden // SEND
    few = count // 8
    piece = count // 2
    pair = z // 2
    partner = z + 1 - 2 * (z % 2)
    near = pair == core
    far_end = jnp.logical_not(near) & ((z == 0) | (z == 3))
    far_mid = jnp.logical_not(near) & ((z == 1) | (z == 2))
    near_mid = near & ((z == 1) | (z == 2))
    onward = 3 - jnp.where(z >= 2, 2, 1)
    first = jnp.where(near, z % 2, 1 - core)
    second = 1 - first

    def loop(steps, body):
        lax.fori_loop(0, steps, lambda i, _: (body(i), 0)[1], 0)

    def span(start, size):
        return pl.ds(pl.multiple_of(start * size, size), size)

    def at(zz, xx, cc):
        return {"row": zz * 2 + xx, "col": cc}

    barrier = pltpu.get_barrier_semaphore()

    def greet(device):
        pl.semaphore_signal(barrier, inc=1, device_id=device, device_id_type=MESH)

    def reach(dz):
        return (z + dz >= 0) & (z + dz <= 3)

    for dz in (1, -1):

        @pl.when(reach(dz))
        def _():
            greet(at(z + dz, x, 0))
            greet(at(z + dz, x, 1))

    greet(at(z, 1 - x, 0))
    greet(at(z, 1 - x, 1))
    greet(at(z, x, 1 - core))

    def load_w(source, zl, n):
        place = (span(zl, depth // 2), span(n, UP))
        return pltpu.make_async_copy(source.at[place], w.at[place], w_sem.at[zl, n])

    def slot(zl, xs, h, q):
        rows = pl.ds(pl.multiple_of(h * count + q * piece, piece), piece)
        return xb.at[zl, rows, span(xs, feats)]

    masks = (
        pltpu.make_async_copy(up_mask, mask_up, mask_sem.at[0]),
        pltpu.make_async_copy(down_mask, mask_down, mask_sem.at[1]),
    )
    for copy in masks:
        copy.start()
    load = pltpu.make_async_copy(
        tokens, xb.at[z % 2, span(core, count), span(x, feats)], load_sem
    )
    pl.when(near)(lambda: load.start())
    loop(ups, lambda n: load_w(w_up, first, n).start())
    loop(ups, lambda n: load_w(w_up, second, n).start())
    sides = jnp.where((z == 0) | (z == 3), 2, 4)
    pl.semaphore_wait(barrier, 3 + sides)

    def send_own(kind, q, device):
        return pltpu.make_async_remote_copy(
            src_ref=tokens.at[pl.ds(q * piece, piece)],
            dst_ref=slot(z % 2, x, core, q),
            send_sem=own_send.at[kind, q], recv_sem=x_recv.at[z % 2, x, core, q],
            device_id=device, device_id_type=MESH,
        )

    def each_own(act):
        for q in (0, 1):
            pl.when(jnp.logical_not(near))(lambda: act(send_own(0, q, at(z, x, pair))))
            act(send_own(1, q, at(z, 1 - x, pair)))
            for kind, dz in ((2, 1), (3, -1)):
                pl.when(reach(dz))(lambda: act(send_own(kind, q, at(z + dz, x, pair))))

    each_own(lambda copy: copy.start())

    def copy_x(kind, zl, xs, h, q, device):
        return pltpu.make_async_remote_copy(
            src_ref=slot(zl, xs, h, q), dst_ref=slot(zl, xs, h, q),
            send_sem=fwd_send.at[kind, zl, h, q], recv_sem=x_recv.at[zl, xs, h, q],
            device_id=device, device_id_type=MESH,
        )

    across, mate = at(z, 1 - x, core), at(z, x, 1 - core)
    end = jnp.where(z >= 2, 3, 0)

    def got(zl, xs, h, q):
        copy_x(0, zl, xs, h, q, across).wait_recv()

    def near_along(q, h):
        got(second, x, h, q)
        pl.when(near_mid)(lambda: copy_x(2, second, x, h, q, at(onward, x, core)).start())
        if q == 0:
            copy_x(0, second, x, h, q, across).start()

    def far_first(q, h):
        got(first, x, h, q)
        pl.when(far_mid)(lambda: copy_x(1, first, x, h, q, at(end, x, core)).start())
        copy_x(0, first, x, h, q, across).start()

    def far_second(q, h):
        got(second, x, h, q)
        pl.when(far_mid)(lambda: copy_x(1, second, x, h, q, at(end, x, core)).start())
        copy_x(0, second, x, h, q, across).start()

    order = ((0, 0), (0, 1), (1, 0), (1, 1))

    def masked(mask, row_at, rows, col_at, wide, mask_row, mask_col):
        parts = []
        for j in range(rows // block):
            place = pl.ds(pl.multiple_of(row_at + j * block, block), block)
            tiles = []
            for t in range(wide // block):
                cols = pl.ds(pl.multiple_of(col_at + t * block, block), block)
                keep = mask[mask_row + j, mask_col + t].astype(F32)
                tiles.append(w[place, cols] * jnp.full((block, block), keep, F32).astype(BF16))
            parts.append(jnp.concatenate(tiles, axis=1))
        return jnp.concatenate(parts, axis=0)

    def up_dot(n, start, rows, xs):
        kept = masked(
            mask_up, start, rows, n * UP, UP, (core * depth + start) // block, n * (UP // block)
        )
        return lax.dot_general(kept, xs, (((0,), (1,)), ((), ())), preferred_element_type=F32)

    def up_start(n):
        load_w(w_up, first, n).wait()
        start = first * (depth // 2) + x * feats
        acc[n] = up_dot(n, start, feats, xb[first, :, span(x, feats)])

    def up_more(n, zl, xs):
        start = zl * (depth // 2) + xs * feats
        acc[n] = acc[n] + up_dot(n, start, feats, xb[zl, :, span(xs, feats)])

    for copy in masks:
        copy.wait()

    @pl.when(near)
    def _():
        load.wait()
        for q in (0, 1):
            got(first, x, 1 - core, q)

    @pl.when(jnp.logical_not(near))
    def _():
        for q, h in order:
            far_first(q, h)

    @pl.when(far_mid)
    def _():
        for q, h in order:
            far_second(q, h)

    def start_forward(n):
        up_start(n)
        for i, (q, h) in enumerate(order):
            pl.when(near & (n == i))(lambda: near_along(q, h))

    loop(ups, start_forward)
    for q, h in order:
        got(first, 1 - x, h, q)

    def with_forward(n):
        up_more(n, first, 1 - x)
        load_w(w_down, first, n).start()
        for i, (q, h) in enumerate(order):
            pl.when(far_end & (n == i))(lambda: far_second(q, h))

    loop(ups, with_forward)
    for h in (0, 1):
        pl.when(near)(lambda: copy_x(1, first, 1 - x, h, 1, at(partner, x, core)).start())

    def up_second(n):
        load_w(w_up, second, n).wait()
        up_more(n, second, x)

    loop(ups, up_second)
    for q, h in order:
        got(second, 1 - x, h, q)

    def half(which):
        return span(which, count)

    def rows_of(n, p):
        return span(2 * n + p, UP // 2)

    def copy_pre(n, p):
        part = span(p, UP // 2)
        return pltpu.make_async_remote_copy(
            src_ref=acc.at[n, part, half(1 - core)], dst_ref=other.at[n, part],
            send_sem=pre_send.at[n, p], recv_sem=pre_recv.at[n, p],
            device_id=mate, device_id_type=MESH,
        )

    def copy_hid(n, p, which):
        place = (rows_of(n, p), half(which))
        return pltpu.make_async_remote_copy(
            src_ref=hid.at[place], dst_ref=hid.at[place],
            send_sem=hid_send.at[n, p], recv_sem=hid_recv.at[n, p],
            device_id=mate, device_id_type=MESH,
        )

    def both(act):
        for p in (0, 1):
            act(p)

    def sent_pre(n):
        both(lambda p: copy_pre(n, p).start())
        load_w(w_down, second, n).start()

    def up_last(n):
        up_more(n, second, 1 - x)
        sent_pre(n)

    def finish(n):
        for p in (0, 1):
            part = pl.ds(p * (UP // 2), UP // 2)
            copy_pre(n, p).wait_recv()
            hid[rows_of(n, p), half(core)] = gelu(
                acc[n, part, half(core)] + other[n, part]
            ).astype(BF16)
            copy_hid(n, p, core).start()

    loop(ups - 1, up_last)
    both(lambda p: copy_pre(0, p).wait_recv())
    up_more(ups - 1, second, 1 - x)
    hid[pl.ds(0, UP), half(core)] = gelu(acc[0, :, half(core)] + other[0]).astype(BF16)
    sent_pre(ups - 1)
    both(lambda p: copy_hid(0, p, core).start())
    loop(ups - 1, lambda n: finish(n + 1))
    loop(ups, lambda n: both(lambda p: copy_hid(n, p, 1 - core).wait_recv()))

    def copy_rx(n):
        return pltpu.make_async_remote_copy(
            src_ref=to_x.at[n], dst_ref=from_x.at[n],
            send_sem=rx_send.at[n], recv_sem=rx_recv.at[n],
            device_id=across, device_id_type=MESH,
        )

    def copy_rz(n, i):
        dz = STEPS[i]
        return pltpu.make_async_remote_copy(
            src_ref=to_z.at[n, jnp.clip(z + dz, 0, 3)], dst_ref=from_z.at[n, i],
            send_sem=rz_send.at[n, i], recv_sem=rz_recv.at[n, i],
            device_id=at(z + dz, x, core), device_id_type=MESH,
        )

    def each_rz(n, act):
        for i, dz in enumerate(STEPS):
            pl.when(reach(dz))(lambda: act(copy_rz(n, i)))

    def down(n):
        for zl in (0, 1):
            pl.when(n % (UP // DOWN) == 0)(lambda: load_w(w_down, zl, n // (UP // DOWN)).wait())
        kept = masked(
            mask_down, 0, depth, n * DOWN, DOWN, 0, (core * downs + n) * (DOWN // block)
        )
        part = lax.dot_general(
            kept, hid[...], (((0,), (0,)), ((), ())), preferred_element_type=F32
        ).T.reshape(2, 4, 2, few, DOWN)
        for s in range(SUBS):
            cols = slice(s * SEND, (s + 1) * SEND)
            for cp in range(2):
                for zp in range(4):
                    pair_of = part[cp, zp, :, :, cols]
                    to_x[n * SUBS + s, zp, cp] = jnp.where(x == 0, pair_of[1], pair_of[0]).astype(BF16)
                    own[n * SUBS + s, zp, cp] = jnp.where(x == 0, pair_of[0], pair_of[1])
            copy_rx(n * SUBS + s).start()

    def take_x(n):
        copy_rx(n).wait_recv()
        total = own[n] + from_x[n].astype(F32)
        own[n] = total
        to_z[n] = total.astype(BF16)
        each_rz(n, lambda copy: copy.start())

    def copy_out(n):
        place = span(core * subs + n, SEND)
        return pltpu.make_async_remote_copy(
            src_ref=final.at[:, span(n, SEND)], dst_ref=out.at[:, place],
            send_sem=out_send.at[n], recv_sem=out_recv.at[n],
            device_id=mate, device_id_type=MESH,
        )

    def finish_out(n):
        for i, dz in enumerate(STEPS):

            @pl.when(reach(-dz))
            def _():
                copy_rz(n, i).wait_recv()
                own[n, z] = own[n, z] + from_z[n, i].astype(F32)

        final[:, span(n, SEND)] = own[n, z, 1 - core].astype(BF16)
        copy_out(n).start()
        out[:, span(core * subs + n, SEND)] = own[n, z, core].astype(BF16)

    def pipeline(i):
        pl.when((i % SUBS == 0) & (i < subs))(lambda: down(i // SUBS))
        for n, stage in ((i - LAG_X, take_x), (i - LAG_Z, finish_out)):
            pl.when((n >= 0) & (n < subs))(functools.partial(stage, n))

    loop(subs + LAG_Z, pipeline)

    each_own(lambda copy: copy.wait_send())
    for q, h in order:

        @pl.when(near)
        def _():
            if q == 1:
                copy_x(1, first, 1 - x, h, q, at(partner, x, core)).wait_send()
            else:
                copy_x(0, second, x, h, q, across).wait_send()
            pl.when(near_mid)(lambda: copy_x(2, second, x, h, q, at(onward, x, core)).wait_send())

        @pl.when(jnp.logical_not(near))
        def _():
            copy_x(0, first, x, h, q, across).wait_send()
            copy_x(0, second, x, h, q, across).wait_send()
            pl.when(far_mid)(lambda: copy_x(1, first, x, h, q, at(end, x, core)).wait_send())
            pl.when(far_mid)(lambda: copy_x(1, second, x, h, q, at(end, x, core)).wait_send())

    def sent_up(n):
        both(lambda p: copy_pre(n, p).wait_send())
        both(lambda p: copy_hid(n, p, core).wait_send())

    loop(ups, sent_up)

    def sent_down(n):
        copy_rx(n).wait_send()
        each_rz(n, lambda copy: copy.wait_send())
        copy_out(n).wait()

    loop(subs, sent_down)


def fused(tokens, w_up, w_down, mask_up, mask_down):
    block = w_up.shape[0] * 2 // mask_up.shape[0]
    count, feats = tokens.shape
    depth, hidden = w_up.shape
    ups, downs = hidden // UP, hidden // DOWN
    few = count // 8
    dma = pltpu.SemaphoreType.DMA
    vmem = pl.BlockSpec(memory_space=pltpu.VMEM)
    hbm = pl.BlockSpec(memory_space=pl.ANY)
    subs = hidden // SEND
    travel = (subs, 4, 2, few, SEND)
    return pl.pallas_call(
        functools.partial(kernel, block),
        out_shape=jax.ShapeDtypeStruct((few, w_down.shape[1] * 2), BF16),
        in_specs=[hbm] * 5,
        out_specs=vmem,
        scratch_shapes=[
            pltpu.SMEM(mask_up.shape, mask_up.dtype),
            pltpu.SMEM(mask_down.shape, mask_down.dtype),
            pltpu.VMEM((depth, hidden), BF16),
            pltpu.VMEM((2, 2 * count, 2 * feats), BF16),
            pltpu.VMEM((ups, UP, 2 * count), F32),
            pltpu.VMEM((ups, UP, count), F32),
            pltpu.VMEM((hidden, 2 * count), BF16),
            pltpu.VMEM(travel, F32),
            pltpu.VMEM(travel, BF16),
            pltpu.VMEM(travel, BF16),
            pltpu.VMEM(travel, BF16),
            pltpu.VMEM((subs, len(STEPS), 2, few, SEND), BF16),
            pltpu.VMEM((few, w_down.shape[1]), BF16),
            dma((2,)),
            dma,
            dma((2, ups)),
            dma((6, 2)),
            dma((3, 2, 2, 2)),
            dma((2, 2, 2, 2)),
            dma((ups, 2)), dma((ups, 2)),
            dma((ups, 2)), dma((ups, 2)),
            dma((subs,)), dma((subs,)),
            dma((subs, len(STEPS))), dma((subs, len(STEPS))),
            dma((subs,)), dma((subs,)),
        ],
        compiler_params=pltpu.CompilerParams(
            collective_id=0, has_side_effects=True, vmem_limit_bytes=63 * 2**20
        ),
    )(tokens, w_up, w_down, mask_up, mask_down)


def per_device(tokens, w_up, w_down, mask_up, mask_down):
    sizes = (lax.axis_size("row"), lax.axis_size("col"))
    square = tokens.shape[1] * 4 == w_up.shape[0] == w_up.shape[1] == w_down.shape[0] == w_down.shape[1]
    if sizes == (8, 2) and square and tokens.shape[0] % 128 == 0 and w_up.shape[1] % UP == 0:
        return fused(tokens, w_up, w_down, mask_up, mask_down)
    return general(tokens, w_up, w_down, mask_up, mask_down)


def solution(mesh):
    return jax.shard_map(
        per_device,
        mesh=mesh,
        in_specs=(
            P(("groups", "col"), "row"),
            P("col", "row"),
            P("row", "col"),
            P(None, "row"),
            P("row", None),
        ),
        out_specs=P(("groups", "col", "row"), None),
        check_vma=False,
    )
```

```python
import functools

import jax
import jax.numpy as jnp
from jax import lax
from jax.experimental import pallas as pl
from jax.experimental.pallas import tpu as pltpu
from jax.sharding import PartitionSpec as P


def expand_mask(mask, block, dtype):
    count_r, count_c = mask.shape
    wide = jnp.broadcast_to(mask.astype(dtype)[:, None, :, None], (count_r, block, count_c, block))
    return wide.reshape(count_r * block, count_c * block)


def general(tokens, w_up, w_down, mask_up, mask_down):
    cols = lax.axis_size("col")
    block = w_up.shape[0] * cols // mask_up.shape[0]
    core = lax.axis_index("col")
    mine = lax.all_gather(tokens, "row", axis=1, tiled=True)
    x = lax.all_to_all(mine, "col", split_axis=1, concat_axis=0, tiled=True)
    half = mask_up.shape[0] // cols
    mask_u = lax.dynamic_slice_in_dim(mask_up, core * half, half, 0)
    pre = jnp.dot(
        x, w_up * expand_mask(mask_u, block, w_up.dtype), preferred_element_type=jnp.float32
    )
    swap = [(i, (i + 1) % cols) for i in range(cols)]
    pre = pre + lax.ppermute(pre.astype(jnp.bfloat16), "col", swap).astype(jnp.float32)
    hidden = jax.nn.gelu(pre, approximate=False).astype(jnp.bfloat16)
    half_d = mask_down.shape[1] // cols
    mask_d = lax.dynamic_slice_in_dim(mask_down, core * half_d, half_d, 1)
    part = jnp.dot(
        hidden,
        w_down * expand_mask(mask_d, block, w_down.dtype),
        preferred_element_type=jnp.float32,
    )
    part = lax.all_to_all(
        part.astype(jnp.bfloat16), "col", split_axis=0, concat_axis=1, tiled=True
    )
    return lax.psum_scatter(part, "row", scatter_dimension=0, tiled=True).astype(jnp.bfloat16)


MESH = pl.DeviceIdType.MESH
BF16, F32 = jnp.bfloat16, jnp.float32
UP, DOWN = 1024, 512
SEND = 512
SUBS = DOWN // SEND
LAG_X, LAG_Z = 2, 5
STEPS = (1, -1, 2, -2, 3, -3)


def gelu(v):
    return 0.5 * v * (1.0 + lax.erf(v * 0.7071067811865476))


def kernel(
    block,
    tokens, w_up, w_down, up_mask, down_mask,
    out,
    mask_up, mask_down, w, xb, acc, other, hid, own, to_x, from_x, to_z, from_z, final,
    mask_sem, load_sem, w_sem, own_send, fwd_send, x_recv, pre_send, pre_recv, hid_send, hid_recv,
    rx_send, rx_recv, rz_send, rz_recv, out_send, out_recv,
):
    row, core = lax.axis_index("row"), lax.axis_index("col")
    z, x = row // 2, row % 2
    count, feats = tokens.shape
    depth, hidden = w.shape
    ups, downs = hidden // UP, hidden // DOWN
    subs = hidden // SEND
    few = count // 8
    piece = count // 2
    pair = z // 2
    partner = z + 1 - 2 * (z % 2)
    near = pair == core
    far_end = jnp.logical_not(near) & ((z == 0) | (z == 3))
    far_mid = jnp.logical_not(near) & ((z == 1) | (z == 2))
    near_mid = near & ((z == 1) | (z == 2))
    onward = 3 - jnp.where(z >= 2, 2, 1)
    first = jnp.where(near, z % 2, 1 - core)
    second = 1 - first

    def loop(steps, body):
        lax.fori_loop(0, steps, lambda i, _: (body(i), 0)[1], 0)

    def span(start, size):
        return pl.ds(pl.multiple_of(start * size, size), size)

    def at(zz, xx, cc):
        return {"row": zz * 2 + xx, "col": cc}

    barrier = pltpu.get_barrier_semaphore()

    def greet(device):
        pl.semaphore_signal(barrier, inc=1, device_id=device, device_id_type=MESH)

    def reach(dz):
        return (z + dz >= 0) & (z + dz <= 3)

    for dz in (1, -1):

        @pl.when(reach(dz))
        def _():
            greet(at(z + dz, x, 0))
            greet(at(z + dz, x, 1))

    greet(at(z, 1 - x, 0))
    greet(at(z, 1 - x, 1))
    greet(at(z, x, 1 - core))

    def load_w(source, zl, n):
        place = (span(zl, depth // 2), span(n, UP))
        return pltpu.make_async_copy(source.at[place], w.at[place], w_sem.at[zl, n])

    def slot(zl, xs, h, q):
        rows = pl.ds(pl.multiple_of(h * count + q * piece, piece), piece)
        return xb.at[zl, rows, span(xs, feats)]

    masks = (
        pltpu.make_async_copy(up_mask, mask_up, mask_sem.at[0]),
        pltpu.make_async_copy(down_mask, mask_down, mask_sem.at[1]),
    )
    for copy in masks:
        copy.start()
    load = pltpu.make_async_copy(
        tokens, xb.at[z % 2, span(core, count), span(x, feats)], load_sem
    )
    pl.when(near)(lambda: load.start())
    loop(ups, lambda n: load_w(w_up, first, n).start())
    loop(ups, lambda n: load_w(w_up, second, n).start())
    sides = jnp.where((z == 0) | (z == 3), 2, 4)
    pl.semaphore_wait(barrier, 3 + sides)

    def send_own(kind, q, device):
        return pltpu.make_async_remote_copy(
            src_ref=tokens.at[pl.ds(q * piece, piece)],
            dst_ref=slot(z % 2, x, core, q),
            send_sem=own_send.at[kind, q], recv_sem=x_recv.at[z % 2, x, core, q],
            device_id=device, device_id_type=MESH,
        )

    def each_own(act):
        for q in (0, 1):
            pl.when(jnp.logical_not(near))(lambda: act(send_own(0, q, at(z, x, pair))))
            act(send_own(1, q, at(z, 1 - x, pair)))
            for kind, dz in ((2, 1), (3, -1)):
                pl.when(reach(dz))(lambda: act(send_own(kind, q, at(z + dz, x, pair))))

    each_own(lambda copy: copy.start())

    def copy_x(kind, zl, xs, h, q, device):
        return pltpu.make_async_remote_copy(
            src_ref=slot(zl, xs, h, q), dst_ref=slot(zl, xs, h, q),
            send_sem=fwd_send.at[kind, zl, h, q], recv_sem=x_recv.at[zl, xs, h, q],
            device_id=device, device_id_type=MESH,
        )

    across, mate = at(z, 1 - x, core), at(z, x, 1 - core)
    end = jnp.where(z >= 2, 3, 0)

    def got(zl, xs, h, q):
        copy_x(0, zl, xs, h, q, across).wait_recv()

    def near_along(q, h):
        got(second, x, h, q)
        pl.when(near_mid)(lambda: copy_x(2, second, x, h, q, at(onward, x, core)).start())
        if q == 0:
            copy_x(0, second, x, h, q, across).start()

    def far_first(q, h):
        got(first, x, h, q)
        pl.when(far_mid)(lambda: copy_x(1, first, x, h, q, at(end, x, core)).start())
        copy_x(0, first, x, h, q, across).start()

    def far_second(q, h):
        got(second, x, h, q)
        pl.when(far_mid)(lambda: copy_x(1, second, x, h, q, at(end, x, core)).start())
        copy_x(0, second, x, h, q, across).start()

    order = ((0, 0), (0, 1), (1, 0), (1, 1))

    def masked(mask, row_at, rows, col_at, wide, mask_row, mask_col):
        parts = []
        for j in range(rows // block):
            place = pl.ds(pl.multiple_of(row_at + j * block, block), block)
            tiles = []
            for t in range(wide // block):
                cols = pl.ds(pl.multiple_of(col_at + t * block, block), block)
                keep = mask[mask_row + j, mask_col + t].astype(F32)
                tiles.append(w[place, cols] * jnp.full((block, block), keep, F32).astype(BF16))
            parts.append(jnp.concatenate(tiles, axis=1))
        return jnp.concatenate(parts, axis=0)

    def up_dot(n, start, rows, xs):
        kept = masked(
            mask_up, start, rows, n * UP, UP, (core * depth + start) // block, n * (UP // block)
        )
        return lax.dot_general(kept, xs, (((0,), (1,)), ((), ())), preferred_element_type=F32)

    def up_start(n):
        load_w(w_up, first, n).wait()
        start = first * (depth // 2) + x * feats
        acc[n] = up_dot(n, start, feats, xb[first, :, span(x, feats)])

    def up_more(n, zl, xs):
        start = zl * (depth // 2) + xs * feats
        acc[n] = acc[n] + up_dot(n, start, feats, xb[zl, :, span(xs, feats)])

    for copy in masks:
        copy.wait()

    @pl.when(near)
    def _():
        load.wait()
        for q in (0, 1):
            got(first, x, 1 - core, q)

    @pl.when(jnp.logical_not(near))
    def _():
        for q, h in order:
            far_first(q, h)

    def start_forward(n):
        up_start(n)
        for i, (q, h) in enumerate(order):
            pl.when(near & (n == i))(lambda: near_along(q, h))
            pl.when(far_mid & (n == i))(lambda: far_second(q, h))

    loop(ups, start_forward)
    for q, h in order:
        got(first, 1 - x, h, q)

    def with_forward(n):
        up_more(n, first, 1 - x)
        load_w(w_down, first, n).start()
        for i, (q, h) in enumerate(order):
            pl.when(far_end & (n == i))(lambda: far_second(q, h))

    loop(ups, with_forward)
    for h in (0, 1):
        pl.when(near)(lambda: copy_x(1, first, 1 - x, h, 1, at(partner, x, core)).start())

    def up_second(n):
        load_w(w_up, second, n).wait()
        up_more(n, second, x)

    loop(ups, up_second)
    for q, h in order:
        got(second, 1 - x, h, q)

    def half(which):
        return span(which, count)

    def copy_pre(n):
        return pltpu.make_async_remote_copy(
            src_ref=acc.at[n, :, half(1 - core)], dst_ref=other.at[n],
            send_sem=pre_send.at[n], recv_sem=pre_recv.at[n],
            device_id=mate, device_id_type=MESH,
        )

    def copy_hid(n, which):
        return pltpu.make_async_remote_copy(
            src_ref=hid.at[span(n, UP), half(which)], dst_ref=hid.at[span(n, UP), half(which)],
            send_sem=hid_send.at[n], recv_sem=hid_recv.at[n],
            device_id=mate, device_id_type=MESH,
        )

    def up_last(n):
        up_more(n, second, 1 - x)
        copy_pre(n).start()
        load_w(w_down, second, n).start()

    def finish(n):
        copy_pre(n).wait_recv()
        hid[span(n, UP), half(core)] = gelu(acc[n, :, half(core)] + other[n]).astype(BF16)
        copy_hid(n, core).start()

    loop(ups, up_last)
    loop(ups, finish)
    loop(ups, lambda n: copy_hid(n, 1 - core).wait_recv())

    def copy_rx(n):
        return pltpu.make_async_remote_copy(
            src_ref=to_x.at[n], dst_ref=from_x.at[n],
            send_sem=rx_send.at[n], recv_sem=rx_recv.at[n],
            device_id=across, device_id_type=MESH,
        )

    def copy_rz(n, i):
        dz = STEPS[i]
        return pltpu.make_async_remote_copy(
            src_ref=to_z.at[n, jnp.clip(z + dz, 0, 3)], dst_ref=from_z.at[n, i],
            send_sem=rz_send.at[n, i], recv_sem=rz_recv.at[n, i],
            device_id=at(z + dz, x, core), device_id_type=MESH,
        )

    def each_rz(n, act):
        for i, dz in enumerate(STEPS):
            pl.when(reach(dz))(lambda: act(copy_rz(n, i)))

    def down(n):
        for zl in (0, 1):
            pl.when(n % (UP // DOWN) == 0)(lambda: load_w(w_down, zl, n // (UP // DOWN)).wait())
        kept = masked(
            mask_down, 0, depth, n * DOWN, DOWN, 0, (core * downs + n) * (DOWN // block)
        )
        part = lax.dot_general(
            kept, hid[...], (((0,), (0,)), ((), ())), preferred_element_type=F32
        ).T.reshape(2, 4, 2, few, DOWN)
        for s in range(SUBS):
            cols = slice(s * SEND, (s + 1) * SEND)
            for cp in range(2):
                for zp in range(4):
                    both = part[cp, zp, :, :, cols]
                    to_x[n * SUBS + s, zp, cp] = jnp.where(x == 0, both[1], both[0]).astype(BF16)
                    own[n * SUBS + s, zp, cp] = jnp.where(x == 0, both[0], both[1])
            copy_rx(n * SUBS + s).start()

    def take_x(n):
        copy_rx(n).wait_recv()
        total = own[n] + from_x[n].astype(F32)
        own[n] = total
        to_z[n] = total.astype(BF16)
        each_rz(n, lambda copy: copy.start())

    def copy_out(n):
        place = span(core * subs + n, SEND)
        return pltpu.make_async_remote_copy(
            src_ref=final.at[:, span(n, SEND)], dst_ref=out.at[:, place],
            send_sem=out_send.at[n], recv_sem=out_recv.at[n],
            device_id=mate, device_id_type=MESH,
        )

    def finish_out(n):
        for i, dz in enumerate(STEPS):

            @pl.when(reach(-dz))
            def _():
                copy_rz(n, i).wait_recv()
                own[n, z] = own[n, z] + from_z[n, i].astype(F32)

        final[:, span(n, SEND)] = own[n, z, 1 - core].astype(BF16)
        copy_out(n).start()
        out[:, span(core * subs + n, SEND)] = own[n, z, core].astype(BF16)

    def pipeline(i):
        pl.when((i % SUBS == 0) & (i < subs))(lambda: down(i // SUBS))
        for n, stage in ((i - LAG_X, take_x), (i - LAG_Z, finish_out)):
            pl.when((n >= 0) & (n < subs))(functools.partial(stage, n))

    loop(subs + LAG_Z, pipeline)

    each_own(lambda copy: copy.wait_send())
    for q, h in order:

        @pl.when(near)
        def _():
            if q == 1:
                copy_x(1, first, 1 - x, h, q, at(partner, x, core)).wait_send()
            else:
                copy_x(0, second, x, h, q, across).wait_send()
            pl.when(near_mid)(lambda: copy_x(2, second, x, h, q, at(onward, x, core)).wait_send())

        @pl.when(jnp.logical_not(near))
        def _():
            copy_x(0, first, x, h, q, across).wait_send()
            copy_x(0, second, x, h, q, across).wait_send()
            pl.when(far_mid)(lambda: copy_x(1, first, x, h, q, at(end, x, core)).wait_send())
            pl.when(far_mid)(lambda: copy_x(1, second, x, h, q, at(end, x, core)).wait_send())

    def sent_up(n):
        copy_pre(n).wait_send()
        copy_hid(n, core).wait_send()

    loop(ups, sent_up)

    def sent_down(n):
        copy_rx(n).wait_send()
        each_rz(n, lambda copy: copy.wait_send())
        copy_out(n).wait()

    loop(subs, sent_down)


def fused(tokens, w_up, w_down, mask_up, mask_down):
    block = w_up.shape[0] * 2 // mask_up.shape[0]
    count, feats = tokens.shape
    depth, hidden = w_up.shape
    ups, downs = hidden // UP, hidden // DOWN
    few = count // 8
    dma = pltpu.SemaphoreType.DMA
    vmem = pl.BlockSpec(memory_space=pltpu.VMEM)
    hbm = pl.BlockSpec(memory_space=pl.ANY)
    subs = hidden // SEND
    travel = (subs, 4, 2, few, SEND)
    return pl.pallas_call(
        functools.partial(kernel, block),
        out_shape=jax.ShapeDtypeStruct((few, w_down.shape[1] * 2), BF16),
        in_specs=[hbm] * 5,
        out_specs=vmem,
        scratch_shapes=[
            pltpu.SMEM(mask_up.shape, mask_up.dtype),
            pltpu.SMEM(mask_down.shape, mask_down.dtype),
            pltpu.VMEM((depth, hidden), BF16),
            pltpu.VMEM((2, 2 * count, 2 * feats), BF16),
            pltpu.VMEM((ups, UP, 2 * count), F32),
            pltpu.VMEM((ups, UP, count), F32),
            pltpu.VMEM((hidden, 2 * count), BF16),
            pltpu.VMEM(travel, F32),
            pltpu.VMEM(travel, BF16),
            pltpu.VMEM(travel, BF16),
            pltpu.VMEM(travel, BF16),
            pltpu.VMEM((subs, len(STEPS), 2, few, SEND), BF16),
            pltpu.VMEM((few, w_down.shape[1]), BF16),
            dma((2,)),
            dma,
            dma((2, ups)),
            dma((6, 2)),
            dma((3, 2, 2, 2)),
            dma((2, 2, 2, 2)),
            dma((ups,)), dma((ups,)),
            dma((ups,)), dma((ups,)),
            dma((subs,)), dma((subs,)),
            dma((subs, len(STEPS))), dma((subs, len(STEPS))),
            dma((subs,)), dma((subs,)),
        ],
        compiler_params=pltpu.CompilerParams(
            collective_id=0, has_side_effects=True, vmem_limit_bytes=63 * 2**20
        ),
    )(tokens, w_up, w_down, mask_up, mask_down)


def per_device(tokens, w_up, w_down, mask_up, mask_down):
    sizes = (lax.axis_size("row"), lax.axis_size("col"))
    square = tokens.shape[1] * 4 == w_up.shape[0] == w_up.shape[1] == w_down.shape[0] == w_down.shape[1]
    if sizes == (8, 2) and square and tokens.shape[0] % 128 == 0 and w_up.shape[1] % UP == 0:
        return fused(tokens, w_up, w_down, mask_up, mask_down)
    return general(tokens, w_up, w_down, mask_up, mask_down)


def solution(mesh):
    return jax.shard_map(
        per_device,
        mesh=mesh,
        in_specs=(
            P(("groups", "col"), "row"),
            P("col", "row"),
            P("row", "col"),
            P(None, "row"),
            P("row", None),
        ),
        out_specs=P(("groups", "col", "row"), None),
        check_vma=False,
    )
```
